32 devices in a mesh: dp: 4 (over z), section: 2 (over core), tensor: 4 (over y, x).
Axes of the slice: x: 2, y: 2, z: 4, core: 2. Of those that a mesh axis runs over, the one named last changes fastest.
Arguments:
- tokens: bfloat16 [1024, 8192], P('dp', 'tensor'), may hold values from -6 to 6
- dest_slot: int32 [1024], P('dp'), may hold values from 0 to 1023, as said below
- doc_reset: int32 [1024], P('dp'), may hold values 0 or 1
- norm_gain: float32 [2, 8192], P('section'), may hold values from 0.25 to 1.75
- w_in: bfloat16 [2, 8192, 5120], P('section', 'dp', 'tensor'), may hold values from -0.0625 to 0.0625
- w_step: bfloat16 [2, 8192, 32], P('section', None, 'tensor'), may hold values from -0.0625 to 0.0625
- step_bias: float32 [2, 32], P('section', 'tensor'), may hold values from -4 to -1.5
- a_log: float32 [2, 32], P('section', 'tensor'), may hold values from -2.5 to 1.5
- d_skip: float32 [2, 32], P('section', 'tensor'), may hold values from 0.3 to 2
- out_gain: float32 [2, 2048], P('section', 'tensor'), may hold values from 0.25 to 1.75
- w_out: bfloat16 [2, 2048, 8192], P('section', 'tensor'), may hold values from -0.125 to 0.125
Outputs:
- phase_out: bfloat16 [2, 1024, 8192], P('section', 'dp', 'tensor')
The draws below stay inside these ranges and needn't reach their ends.
Inputs may be any that keep to these rules, and one draw needn't show every extreme that they name: dest_slot is a permutation; the tokens of one group go in order to increasing groups, and each group receives rows in order of source group. One group sends at most 128 tokens to one group, and every group sends exactly 128 to some group.
All inputs are finite; a program needn't handle non-finite values. No bound on the sum of `doc_reset` on one device may be relied on, other than what follows from the above.
Results may differ from the reference program's by a relative error of at most 0.018.
Values may be sent and summed in bfloat16 or wider, within the bound.
A program may use at most 128 MiB of HBM per device.

```python
import jax
import jax.numpy as jnp
from jax import lax

D = 8192
HEAD_DIM = 64
STATE = 128
HEADS_DEV = 8
SPAN = 64
ROWS = 256
HEADS = 32
TOKENS = 1024
COLS = 5120
N_DP = 4
N_SECTION = 2
N_TENSOR = 4


def draw_dest_slot(key, part):
    share = ROWS // N_DP
    key_order = jax.random.fold_in(key, 7101)
    key_shift = jax.random.fold_in(key, 7203)
    scores = jax.random.randint(key_order, (N_DP,), 0, 1 << 20) * N_DP + jnp.arange(N_DP)
    sigma = jnp.argsort(scores).astype(jnp.int32)
    offset = jax.random.randint(key_shift, (), 1, N_DP)
    source = jnp.arange(N_DP)
    plus_to = sigma
    minus_to = sigma[(source + offset) % N_DP]
    target = jnp.arange(N_DP)[None, :]
    counts = share + share * (target == plus_to[:, None]).astype(jnp.int32) - share * (target == minus_to[:, None]).astype(jnp.int32)
    ends = jnp.cumsum(counts, axis=1)
    starts = ends - counts
    earlier = jnp.cumsum(counts, axis=0) - counts
    everyrow = jnp.arange(ROWS * N_DP)
    src_group = everyrow // ROWS
    within_src = everyrow % ROWS
    dst_group = jnp.sum((ends[src_group] <= within_src[:, None]).astype(jnp.int32), axis=1)
    within_dst = within_src - starts[src_group, dst_group]
    return (dst_group * ROWS + earlier[src_group, dst_group] + within_dst).astype(jnp.int32)


def set_ends(result, rng, smallest, top_value):
    dims = result.shape
    index_at = [jax.random.randint(jax.random.fold_in(rng, axis), (), 0, dims[axis]) for axis in range(len(dims))]
    result = result.at[tuple(index_at)].set(smallest)
    longest = dims.index(max(dims))
    index_at[longest] = (index_at[longest] + 1) % dims[longest]
    return result.at[tuple(index_at)].set(top_value)


def shard_levels(rng, shape, cuts, smallest, largest):
    level = 1.0
    for axis_at, blocks in cuts:
        heights = jax.random.uniform(jax.random.fold_in(jax.random.fold_in(rng, 6), axis_at), (blocks,), jnp.float32, smallest / len(cuts), largest / len(cuts))
        level = level * jnp.repeat(jnp.exp(heights), shape[axis_at] // blocks).reshape((-1,) + (1,) * (len(shape) - 1 - axis_at))
    return level


def bell_draw(rng, extent, deviation, reach, cuts=(), held_as=jnp.bfloat16):
    entries = jax.random.normal(rng, extent, jnp.float32) * deviation
    if len(cuts) > 0:
        entries = shard_levels(rng, extent, cuts, -0.22, 0.18) * entries
    return jnp.clip(entries, min=-reach, max=reach).astype(held_as)


def setup_inputs(seed: int = 0) -> dict:
    key_of = jax.random.split(jax.random.key(seed), 12)
    tokens = bell_draw(key_of[0], (TOKENS, D), 1.0, 6.0, ((0, 4), (1, 4)))
    dest_slot = draw_dest_slot(jax.random.fold_in(key_of[11], 71), 0)
    doc_reset = set_ends((jax.random.randint(key_of[2], (TOKENS,), 0, 48) < 1).astype(jnp.int32), jax.random.fold_in(key_of[2], 1), 0, 1)
    norm_gain = jnp.clip(1.0 + 0.15 * jax.random.normal(key_of[3], (N_SECTION, D), jnp.float32), 0.25, 1.75)
    w_in = bell_draw(key_of[4], (N_SECTION, D, COLS), D ** -0.5, 0.0625, ((0, 2), (1, 4), (2, 4)))
    w_step = bell_draw(key_of[5], (N_SECTION, D, HEADS), D ** -0.5, 0.0625, ((0, 2), (2, 4)))
    step_bias = jnp.clip(-4.0 + 2.5 * jax.random.uniform(key_of[6], (N_SECTION, HEADS), jnp.float32) ** shard_levels(key_of[6], (N_SECTION, HEADS), ((0, 2), (1, 4)), -0.2, 0.2), -4.0, -1.5)
    a_log = jnp.clip(-2.5 + 4.0 * jax.random.uniform(key_of[7], (N_SECTION, HEADS), jnp.float32) ** shard_levels(key_of[7], (N_SECTION, HEADS), ((0, 2), (1, 4)), -0.2, 0.2), -2.5, 1.5)
    d_skip = jnp.clip(0.3 + 1.7 * jax.random.uniform(key_of[8], (N_SECTION, HEADS), jnp.float32) ** shard_levels(key_of[8], (N_SECTION, HEADS), ((0, 2), (1, 4)), -0.2, 0.2), 0.3, 2.0)
    out_gain = jnp.clip(1.0 + 0.15 * jax.random.normal(key_of[9], (N_SECTION, HEADS * HEAD_DIM), jnp.float32), 0.25, 1.75)
    w_out = bell_draw(key_of[10], (N_SECTION, HEADS * HEAD_DIM, D), (HEADS * HEAD_DIM) ** -0.5, 0.125, ((0, 2), (1, 4)))
    return dict(tokens=tokens, dest_slot=dest_slot, doc_reset=doc_reset, norm_gain=norm_gain, w_in=w_in, w_step=w_step, step_bias=step_bias, a_log=a_log, d_skip=d_skip, out_gain=out_gain, w_out=w_out)


epsilon = 1e-05

def scan_block(inputs, writes, readout, step_size, log_decay, resets, state, skips):
    hp = lax.Precision.HIGHEST
    segment = jnp.cumsum(resets)
    cumulative = jnp.cumsum(log_decay, axis=0)
    positions = jnp.arange(resets.shape[0])
    in_segment = (segment[:, None] == segment[None, :]) & (positions[:, None] >= positions[None, :])
    gap = cumulative[:, None, :] - cumulative[None, :, :]
    decayed = jnp.where(in_segment[:, :, None], jnp.exp(jnp.where(in_segment[:, :, None], gap, 0.0)), 0.0)
    scores = jnp.einsum('thn,shn->tsh', readout, writes, precision=hp)
    weights = scores * decayed * step_size[None, :, :]
    output = jnp.einsum('tsh,shp->thp', weights, inputs, precision=hp)
    carry_ok = (segment == 0).astype(inputs.dtype)
    carried = jnp.einsum('thn,hpn->thp', readout, state, precision=hp)
    output = output + carry_ok[:, None, None] * jnp.exp(cumulative)[:, :, None] * carried
    last_seg = segment[-1]
    tail = (segment == last_seg).astype(inputs.dtype)[:, None] * jnp.exp(cumulative[-1][None, :] - cumulative) * step_size
    fresh = jnp.einsum('sh,shp,shn->hpn', tail, inputs, writes, precision=hp)
    kept = (last_seg == 0).astype(inputs.dtype) * jnp.exp(cumulative[-1])[:, None, None] * state
    output = output + skips[None, :, None] * inputs
    return (output, fresh + kept)

def scan_group(inputs, writes, readout, step_size, log_decay, resets, skips):
    blocks = ROWS // SPAN

    def split(arr):
        return arr.reshape((blocks, SPAN) + arr.shape[1:])

    def stepper(state, pieces):
        output, fresh = scan_block(*pieces, state, skips)
        return (fresh, output)
    start = jnp.zeros((HEADS, HEAD_DIM, STATE), inputs.dtype)
    _, outputs = lax.scan(stepper, start, (split(inputs), split(writes), split(readout), split(step_size), split(log_decay), split(resets)))
    return outputs.reshape((ROWS,) + outputs.shape[2:])

def reference(tokens, dest_slot, doc_reset, norm_gain, w_in, w_step, step_bias, a_log, d_skip, out_gain, w_out):
    per_block = 2 * HEADS_DEV * HEAD_DIM + 2 * STATE
    head_cols = HEADS_DEV * HEAD_DIM
    hidden = jnp.zeros_like(tokens).at[dest_slot].set(tokens)
    results = []
    for layer_idx in range(N_SECTION):
        widened = hidden.astype(jnp.float32)
        meansq = lax.optimization_barrier(jnp.mean(widened * widened, axis=-1, keepdims=True))
        normed_in = (widened * lax.rsqrt(meansq + epsilon) * norm_gain[layer_idx]).astype(jnp.bfloat16)
        proj = jnp.dot(normed_in, w_in[layer_idx], preferred_element_type=jnp.float32).astype(jnp.bfloat16)
        proj = proj.reshape(TOKENS, N_TENSOR, per_block)
        gate_proj = proj[:, :, :head_cols].astype(jnp.float32)
        inputs = proj[:, :, head_cols:2 * head_cols].astype(jnp.float32).reshape(TOKENS, HEADS, HEAD_DIM)
        writes = jnp.repeat(proj[:, :, 2 * head_cols:2 * head_cols + STATE].astype(jnp.float32), HEADS_DEV, axis=1)
        readout = jnp.repeat(proj[:, :, 2 * head_cols + STATE:].astype(jnp.float32), HEADS_DEV, axis=1)
        step_size = jax.nn.softplus(jnp.dot(normed_in, w_step[layer_idx], preferred_element_type=jnp.float32) + step_bias[layer_idx])
        log_decay = -jnp.exp(a_log[layer_idx]) * step_size

        def grouped(arr):
            return arr.reshape((N_DP, ROWS) + arr.shape[1:])
        mixed = jax.vmap(scan_group, in_axes=(0, 0, 0, 0, 0, 0, None))(grouped(inputs), grouped(writes), grouped(readout), grouped(step_size), grouped(log_decay), grouped(doc_reset), d_skip[layer_idx])
        mixed = mixed.reshape(TOKENS, N_TENSOR, head_cols)
        gated = mixed * jax.nn.silu(gate_proj)
        meansq_out = lax.optimization_barrier(jnp.mean(gated * gated, axis=-1, keepdims=True))
        normed = (gated * lax.rsqrt(meansq_out + epsilon) * out_gain[layer_idx].reshape(N_TENSOR, head_cols)).astype(jnp.bfloat16)
        summed = jnp.zeros((TOKENS, D), jnp.float32)
        for block_idx in range(N_TENSOR):
            rows_w = w_out[layer_idx][block_idx * head_cols:(block_idx + 1) * head_cols]
            partial_value = jnp.dot(normed[:, block_idx, :], rows_w, preferred_element_type=jnp.float32).astype(jnp.bfloat16)
            summed = summed + lax.optimization_barrier(partial_value).astype(jnp.float32)
        hidden = (widened + summed).astype(jnp.bfloat16)
        results.append(hidden)
    return jnp.stack(results)
```

```python
import jax
import jax.numpy as jnp
from jax import lax
from jax.sharding import PartitionSpec as P

HEAD_DIM = 64
STATE = 128
HEADS_DEV = 8
SPAN = 64


epsilon = 1e-05


def scan_block(inputs, writes, readout, step_size, log_decay, resets, state, skips):
    segment = jnp.cumsum(resets)
    cumulative = jnp.cumsum(log_decay, axis=0)
    positions = jnp.arange(resets.shape[0])
    in_segment = (segment[:, None] == segment[None, :]) & (positions[:, None] >= positions[None, :])
    by_head = cumulative.T
    gap = by_head[:, :, None] - by_head[:, None, :]
    decayed = jnp.where(in_segment[None], jnp.exp(jnp.where(in_segment[None], gap, 0.0)), 0.0)
    f32 = jnp.float32
    scores = jnp.einsum("tn,sn->ts", readout, writes, preferred_element_type=f32)
    weights = scores[None] * decayed * step_size.T[:, None, :]
    output = jnp.einsum("hts,shp->thp", weights, inputs.astype(f32))
    carry_ok = (segment == 0).astype(f32)
    carried = jnp.einsum("tn,hpn->thp", readout.astype(f32), state)
    output = output + carry_ok[:, None, None] * jnp.exp(cumulative)[:, :, None] * carried
    last_seg = segment[-1]
    tail = (
        (segment == last_seg).astype(f32)[:, None]
        * jnp.exp(cumulative[-1][None, :] - cumulative)
        * step_size
    )
    fresh = jnp.einsum("shp,sn->hpn", tail[:, :, None] * inputs.astype(f32), writes.astype(f32))
    kept = (last_seg == 0).astype(f32) * jnp.exp(cumulative[-1])[:, None, None] * state
    output = output + skips[None, :, None] * inputs.astype(f32)
    return (output, fresh + kept)


def per_device(
    tokens, dest_slot, doc_reset, norm_gain, w_in, w_step, step_bias, a_log, d_skip, out_gain, w_out
):
    f32, bf16 = jnp.float32, jnp.bfloat16
    groups = lax.axis_size("dp")
    width = lax.axis_size("tensor")
    cores = lax.axis_size("section")
    layers = cores
    dp_idx = lax.axis_index("dp")
    core = lax.axis_index("section")
    row_count = tokens.shape[0]
    feat_local = tokens.shape[1]
    feats = feat_local * width
    capacity = 2 * row_count // groups
    head_cols = HEADS_DEV * HEAD_DIM

    def whole(param):
        return lax.all_gather(param, "section", axis=0, tiled=True)

    w_in, w_out, w_step = whole(w_in), whole(w_out), whole(w_step)
    norm_gain, step_bias, a_log, d_skip, out_gain = (
        whole(norm_gain), whole(step_bias), whole(a_log), whole(d_skip), whole(out_gain)
    )

    part = feat_local // cores
    mine = lax.dynamic_slice_in_dim(tokens, core * part, part, axis=1)
    target = dest_slot // row_count
    onehot = (target[:, None] == jnp.arange(groups)[None, :]).astype(jnp.int32)
    before = jnp.cumsum(onehot, axis=0) - onehot
    placed = jnp.sum(onehot * before, axis=1)
    slots = target * capacity + placed
    outbox = jnp.zeros((groups * capacity, part), bf16).at[slots].set(mine)
    marks = (
        jnp.full((groups * capacity,), row_count, jnp.int32).at[slots].set(dest_slot % row_count)
    )
    inbox = lax.all_to_all(
        outbox.reshape(groups, capacity, part), "dp", split_axis=0, concat_axis=0, tiled=True
    )
    where_to = lax.all_to_all(
        marks.reshape(groups, capacity), "dp", split_axis=0, concat_axis=0, tiled=True
    )
    balanced = (
        jnp.zeros((row_count, part), bf16)
        .at[where_to.reshape(-1)]
        .set(inbox.reshape(-1, part), mode="drop")
    )
    few = row_count // (cores * width)
    half = row_count // cores
    rows = lax.all_to_all(
        balanced.reshape(cores * width, few, part), ("section", "tensor"), 0, 0, tiled=True
    )
    rows = rows.reshape(cores, width, few, part).transpose(2, 1, 0, 3).reshape(few, feats)

    depth = w_in.shape[1]
    outs = []
    for layer in range(layers):
        widened = rows.astype(f32)
        meansq = jnp.mean(widened * widened, axis=-1, keepdims=True)
        u = (widened * lax.rsqrt(meansq + epsilon) * norm_gain[layer]).astype(bf16)
        u = u.reshape(few, groups, depth).transpose(1, 0, 2)
        u = lax.all_to_all(u, "dp", 0, 0, tiled=True)
        step_w = lax.dynamic_slice_in_dim(w_step[layer], dp_idx * depth, depth, axis=0)
        full_u = lax.all_gather(u, "tensor", axis=1, tiled=True)
        full_u = full_u.reshape(groups * half, depth)
        proj = jnp.dot(full_u, w_in[layer], preferred_element_type=f32).astype(bf16)
        pre = jnp.dot(full_u, step_w, preferred_element_type=f32)
        proj = lax.all_to_all(proj.reshape(groups, half, -1), "dp", 0, 0, tiled=True)
        pre = lax.all_to_all(pre.reshape(groups, half, HEADS_DEV), "dp", 0, 0, tiled=True)
        proj = jnp.sum(proj.astype(f32), axis=0).astype(bf16)
        pre = jnp.sum(pre, axis=0)
        proj = lax.all_gather(proj, "section", axis=0, tiled=True)
        pre = lax.all_gather(pre, "section", axis=0, tiled=True)
        step_size = jax.nn.softplus(pre + step_bias[layer])
        log_decay = -jnp.exp(a_log[layer]) * step_size
        state = jnp.zeros((HEADS_DEV, HEAD_DIM, STATE), f32)
        mixed = []
        for at in range(0, row_count, SPAN):
            span = slice(at, at + SPAN)
            output, state = scan_block(
                proj[span, head_cols : 2 * head_cols].reshape(SPAN, HEADS_DEV, HEAD_DIM),
                proj[span, 2 * head_cols : 2 * head_cols + STATE],
                proj[span, 2 * head_cols + STATE :],
                step_size[span],
                log_decay[span],
                doc_reset[span],
                state,
                d_skip[layer],
            )
            mixed.append(output.reshape(SPAN, head_cols))
        mixed = jnp.concatenate(mixed, axis=0)
        mixed = lax.dynamic_slice_in_dim(mixed, core * half, half, axis=0)
        gate = lax.dynamic_slice_in_dim(proj[:, :head_cols], core * half, half, axis=0).astype(f32)
        gated = mixed * jax.nn.silu(gate)
        meansq_out = jnp.mean(gated * gated, axis=-1, keepdims=True)
        normed = (gated * lax.rsqrt(meansq_out + epsilon) * out_gain[layer]).astype(bf16)
        partial_value = jnp.dot(normed, w_out[layer], preferred_element_type=f32).astype(bf16)
        partial_value = lax.all_to_all(
            partial_value.reshape(width, few, feats), "tensor", 0, 0, tiled=True
        )
        summed = jnp.sum(partial_value.astype(f32), axis=0)
        rows = (widened + summed).astype(bf16)
        outs.append(rows.reshape(few, width, feat_local).transpose(1, 0, 2))
    outs = jnp.concatenate(outs, axis=0)
    outs = lax.all_to_all(outs, ("section", "tensor"), 0, 0, tiled=True)
    return outs.reshape(1, row_count, feat_local)


def solution(mesh):
    placed = (
        P("dp", "tensor"),
        P("dp"),
        P("dp"),
        P("section", None),
        P("section", "dp", "tensor"),
        P("section", None, "tensor"),
        P("section", "tensor"),
        P("section", "tensor"),
        P("section", "tensor"),
        P("section", "tensor"),
        P("section", "tensor", None),
    )
    return jax.shard_map(
        per_device,
        mesh=mesh,
        in_specs=placed,
        out_specs=P("section", "dp", "tensor"),
        check_vma=False,
    )
```

```python
import jax
import jax.numpy as jnp
from jax import lax
from jax.sharding import PartitionSpec as P

HEAD_DIM = 64
STATE = 128
HEADS_DEV = 8


epsilon = 1e-05


def scan_block(inputs, writes, readout, step_size, log_decay, resets, state, skips):
    segment = jnp.cumsum(resets)
    cumulative = jnp.cumsum(log_decay, axis=0)
    positions = jnp.arange(resets.shape[0])
    in_segment = (segment[:, None] == segment[None, :]) & (positions[:, None] >= positions[None, :])
    by_head = cumulative.T
    gap = by_head[:, :, None] - by_head[:, None, :]
    decayed = jnp.where(in_segment[None], jnp.exp(jnp.where(in_segment[None], gap, 0.0)), 0.0)
    f32 = jnp.float32
    scores = jnp.einsum("tn,sn->ts", readout, writes, preferred_element_type=f32)
    weights = scores[None] * decayed * step_size.T[:, None, :]
    output = jnp.einsum("hts,shp->thp", weights, inputs.astype(f32))
    carry_ok = (segment == 0).astype(f32)
    carried = jnp.einsum("tn,hpn->thp", readout.astype(f32), state)
    output = output + carry_ok[:, None, None] * jnp.exp(cumulative)[:, :, None] * carried
    last_seg = segment[-1]
    tail = (
        (segment == last_seg).astype(f32)[:, None]
        * jnp.exp(cumulative[-1][None, :] - cumulative)
        * step_size
    )
    fresh = jnp.einsum("shp,sn->hpn", tail[:, :, None] * inputs.astype(f32), writes.astype(f32))
    kept = (last_seg == 0).astype(f32) * jnp.exp(cumulative[-1])[:, None, None] * state
    output = output + skips[None, :, None] * inputs.astype(f32)
    return (output, fresh + kept)


CHUNKS = 2


def shift(block, axis, distance):
    n = lax.axis_size(axis)
    return lax.ppermute(block, axis, [(i, (i + distance) % n) for i in range(n)])


def exchange(blocks, axis):
    return [b if k == 0 else shift(b, axis, k) for k, b in enumerate(blocks)]


def turned(stack, start):
    n = stack.shape[0]
    return lax.dynamic_slice_in_dim(jnp.concatenate([stack, stack], axis=0), start, n, axis=0)


def in_order(stack, me):
    n = stack.shape[0]
    return turned(stack[::-1], n - 1 - me)


def per_device(
    tokens, dest_slot, doc_reset, norm_gain, w_in, w_step, step_bias, a_log, d_skip, out_gain, w_out
):
    f32, bf16 = jnp.float32, jnp.bfloat16
    groups = lax.axis_size("dp")
    width = lax.axis_size("tensor")
    cores = lax.axis_size("section")
    group, lane, core = lax.axis_index("dp"), lax.axis_index("tensor"), lax.axis_index("section")
    row_count, feat_local = tokens.shape
    feats = feat_local * width
    depth = w_in.shape[1]
    head_cols = HEADS_DEV * HEAD_DIM
    half = row_count // cores
    src_few = half // width
    few = half // (CHUNKS * width)
    part = few * width

    w_in = lax.all_gather(w_in, "section", axis=0, tiled=True)
    step_own = lax.dynamic_slice_in_dim(w_step[0], group * depth, depth, axis=0)
    w_step = lax.all_gather(step_own, "section", axis=0)
    small = [norm_gain[0], step_bias[0], a_log[0], d_skip[0], out_gain[0]]
    joined = lax.all_gather(jnp.concatenate(small), "section", axis=0)
    params, at = [], 0
    for piece in small:
        params.append(joined[:, at : at + piece.shape[0]])
        at += piece.shape[0]
    norm_gain, step_bias, a_log, d_skip, out_gain = params
    w_out = lax.all_gather(w_out, "section", axis=0, tiled=True)

    mine = lax.dynamic_slice_in_dim(tokens, core * half, half, axis=0)
    mine = lax.all_to_all(mine.reshape(width, src_few, feat_local), "tensor", 0, 0, tiled=True)
    mine = mine.transpose(1, 0, 2).reshape(src_few, groups, depth).transpose(1, 0, 2)
    mine = lax.all_to_all(mine, "dp", 0, 0, tiled=True)
    parts = exchange([mine] * width, "tensor")
    others = [shift(p, "section", 1) for p in parts]
    pool = jnp.stack(parts + others).reshape(-1, depth)

    slots = lax.all_gather(dest_slot, "dp", axis=0, tiled=True)
    source_of = jnp.zeros_like(slots).at[slots].set(jnp.arange(slots.shape[0], dtype=jnp.int32))
    source_of = source_of.reshape(groups, CHUNKS, cores, part)
    source_of = lax.dynamic_index_in_dim(source_of, core, 2, keepdims=False)
    source_of = turned(source_of, group).transpose(1, 0, 2)
    src_group, inner = source_of // row_count, source_of % row_count
    src_core, inner = inner // half, inner % half
    src_lane, inner = inner // src_few, inner % src_few
    place = (core - src_core) % cores * width + (lane - src_lane) % width
    place = (place * groups + src_group) * src_few + inner
    first = pool[place.reshape(-1)].reshape(CHUNKS, groups, part, depth)
    gain_own = lax.dynamic_slice_in_dim(norm_gain[0], group * depth, depth)

    def project(rows, layer):
        flat = rows.reshape(groups * part, depth)
        proj = jnp.dot(flat, w_in[layer], preferred_element_type=f32).astype(bf16)
        pre = jnp.dot(flat, w_step[layer], preferred_element_type=f32)
        return proj.reshape(groups, part, -1), pre.reshape(groups, part, -1)

    def added(blocks):
        return sum(b.astype(f32) for b in blocks)

    def mix(proj, pre, resets, state, layer):
        proj = lax.all_gather(proj, "section", axis=0, tiled=True)
        pre = lax.all_gather(pre, "section", axis=0, tiled=True)
        count = proj.shape[0]
        step_size = jax.nn.softplus(pre + step_bias[layer])
        log_decay = -jnp.exp(a_log[layer]) * step_size
        mixed, state = scan_block(
            proj[:, head_cols : 2 * head_cols].reshape(count, HEADS_DEV, HEAD_DIM),
            proj[:, 2 * head_cols : 2 * head_cols + STATE],
            proj[:, 2 * head_cols + STATE :],
            step_size,
            log_decay,
            resets,
            state,
            d_skip[layer],
        )
        mixed = mixed.reshape(count, head_cols)
        mixed = lax.dynamic_slice_in_dim(mixed, core * part, part, axis=0)
        gate = lax.dynamic_slice_in_dim(proj[:, :head_cols], core * part, part, axis=0).astype(f32)
        gated = mixed * jax.nn.silu(gate)
        meansq_out = jnp.mean(gated * gated, axis=-1, keepdims=True)
        normed = (gated * lax.rsqrt(meansq_out + epsilon) * out_gain[layer]).astype(bf16)
        normed = turned(normed.reshape(width, few, head_cols), lane).reshape(part, head_cols)
        partial_value = jnp.dot(normed, w_out[layer], preferred_element_type=f32).astype(bf16)
        blocks = partial_value.reshape(width, few, feats)
        return added(exchange([blocks[k] for k in range(width)], "tensor")), state

    def delivered(rows, layer):
        blocks = turned(rows.reshape(few, width, feat_local).transpose(1, 0, 2), lane)
        own = jnp.stack(exchange([blocks[k] for k in range(width)], "tensor"))
        own = in_order(own, lane).reshape(part, feat_local)
        return own, lax.ppermute(own, "section", [(cores - 1 - layer, layer)])

    resets = doc_reset.reshape(CHUNKS, -1)
    zero_state = jnp.zeros((HEADS_DEV, HEAD_DIM, STATE), f32)
    sent = []
    for c in range(CHUNKS):
        wide = first[c].astype(f32)
        squares = jnp.sum(wide * wide, axis=-1)
        proj, pre = project((wide * gain_own).astype(bf16), 0)
        side = jnp.concatenate([pre, squares[:, :, None]], axis=-1)
        kept = lax.dynamic_slice_in_dim(first[c], lane * few, few, axis=1)
        proj = exchange([proj[k] for k in range(groups)], "dp")
        side = exchange([side[k] for k in range(groups)], "dp")
        kept = exchange([kept[k] for k in range(groups)], "dp")
        sent.append((proj, side, kept))
    state = zero_state
    middle, outs = [], []
    for c in range(CHUNKS):
        proj, side, kept = sent[c]
        side = added(side)
        scale = lax.rsqrt(side[:, HEADS_DEV:] / feats + epsilon)
        summed, state = mix(
            (added(proj) * scale).astype(bf16), side[:, :HEADS_DEV] * scale, resets[c], state, 0
        )
        kept = in_order(jnp.stack(kept), group).transpose(1, 0, 2).reshape(few, feats)
        rows = (kept.astype(f32) + summed).astype(bf16)
        middle.append(rows)
        widened = rows.astype(f32)
        meansq = jnp.mean(widened * widened, axis=-1, keepdims=True)
        u = (widened * lax.rsqrt(meansq + epsilon) * norm_gain[1]).astype(bf16)
        u = turned(u.reshape(few, groups, depth).transpose(1, 0, 2), group)
        u = jnp.stack(exchange([u[k] for k in range(groups)], "dp"))
        u = jnp.stack(exchange([u] * width, "tensor"), axis=1)
        proj, pre = project(u, 1)
        back = [(groups - k) % groups for k in range(groups)]
        proj = exchange([proj[k] for k in back], "dp")
        pre = exchange([pre[k] for k in back], "dp")
        sent[c] = (proj, pre)
    state = zero_state
    for c in range(CHUNKS):
        proj, pre = sent[c]
        proj = in_order(added(proj).astype(bf16).reshape(width, few, -1), lane).reshape(part, -1)
        pre = in_order(added(pre).reshape(width, few, -1), lane).reshape(part, -1)
        summed, state = mix(proj, pre, resets[c], state, 1)
        rows = (middle[c].astype(f32) + summed).astype(bf16)
        own_a, got_a = delivered(middle[c], 0)
        own_b, got_b = delivered(rows, 1)
        outs.append(jnp.where(core == 0, own_a, got_b))
        outs.append(jnp.where(core == 0, got_a, own_b))
    return jnp.concatenate(outs, axis=0)[None]


def solution(mesh):
    placed = (
        P("dp", "tensor"),
        P("dp"),
        P("dp"),
        P("section", None),
        P("section", "dp", "tensor"),
        P("section", None, "tensor"),
        P("section", "tensor"),
        P("section", "tensor"),
        P("section", "tensor"),
        P("section", "tensor"),
        P("section", "tensor", None),
    )
    return jax.shard_map(
        per_device,
        mesh=mesh,
        in_specs=placed,
        out_specs=P("section", "dp", "tensor"),
        check_vma=False,
    )
```

```python
import jax
import jax.numpy as jnp
from jax import lax
from jax.experimental import pallas as pl
from jax.experimental.pallas import tpu as pltpu
from jax.sharding import PartitionSpec as P

HEAD_DIM = 64
STATE = 128
HEADS_DEV = 8


epsilon = 1e-05


def scan_block(inputs, writes, readout, step_size, log_decay, resets, state, skips):
    segment = jnp.cumsum(resets)
    cumulative = jnp.cumsum(log_decay, axis=0)
    positions = jnp.arange(resets.shape[0])
    in_segment = (segment[:, None] == segment[None, :]) & (positions[:, None] >= positions[None, :])
    by_head = cumulative.T
    gap = by_head[:, :, None] - by_head[:, None, :]
    decayed = jnp.where(in_segment[None], jnp.exp(jnp.where(in_segment[None], gap, 0.0)), 0.0)
    f32 = jnp.float32
    scores = jnp.einsum("tn,sn->ts", readout, writes, preferred_element_type=f32)
    weights = scores[None] * decayed * step_size.T[:, None, :]
    output = jnp.einsum("hts,shp->thp", weights, inputs.astype(f32))
    carry_ok = (segment == 0).astype(f32)
    carried = jnp.einsum("tn,hpn->thp", readout.astype(f32), state)
    output = output + carry_ok[:, None, None] * jnp.exp(cumulative)[:, :, None] * carried
    last_seg = segment[-1]
    tail = (
        (segment == last_seg).astype(f32)[:, None]
        * jnp.exp(cumulative[-1][None, :] - cumulative)
        * step_size
    )
    fresh = jnp.einsum("shp,sn->hpn", tail[:, :, None] * inputs.astype(f32), writes.astype(f32))
    kept = (last_seg == 0).astype(f32) * jnp.exp(cumulative[-1])[:, None, None] * state
    output = output + skips[None, :, None] * inputs.astype(f32)
    return (output, fresh + kept)


CHUNKS = 2


MESH = pl.DeviceIdType.MESH


def greet(peers):
    barrier = pltpu.get_barrier_semaphore()
    for peer in peers:
        pl.semaphore_signal(barrier, inc=1, device_id=peer, device_id_type=MESH)
    pl.semaphore_wait(barrier, len(peers))


def remote_call(kernel, out_shape, operands, n_sems, collective_id):
    anywhere = pl.BlockSpec(memory_space=pl.ANY)
    sems = [pltpu.SemaphoreType.DMA((n_sems,)), pltpu.SemaphoreType.DMA((n_sems,))]
    return pl.pallas_call(
        kernel,
        out_shape=out_shape,
        in_specs=[anywhere] * len(operands),
        out_specs=[anywhere] * len(out_shape),
        scratch_shapes=sems,
        compiler_params=pltpu.CompilerParams(collective_id=collective_id, has_side_effects=True),
    )(*operands)


def exchange(jobs, collective_id):
    sizes = [lax.axis_size(axis) for _, axis, _ in jobs]
    operands = [array for array, _, _ in jobs]
    out_shape = []
    for (array, _, spread), n in zip(jobs, sizes):
        block = array.shape if spread else array.shape[1:]
        out_shape.append(jax.ShapeDtypeStruct((n - 1,) + block, array.dtype))
    axes = sorted({axis for _, axis, _ in jobs})
    n_sems = sum(n - 1 for n in sizes)

    def kernel(*refs):
        sources, targets = refs[: len(jobs)], refs[len(jobs) : 2 * len(jobs)]
        send_sem, recv_sem = refs[2 * len(jobs) :]
        peers = []
        for axis in axes:
            n = lax.axis_size(axis)
            peers += [{axis: lax.rem(lax.axis_index(axis) + k, n)} for k in range(1, n)]
        greet(peers)
        copies = []
        for (_, axis, spread), n, source, target in zip(jobs, sizes, sources, targets):
            for k in range(1, n):
                copy = pltpu.make_async_remote_copy(
                    src_ref=source if spread else source.at[k],
                    dst_ref=target.at[k - 1],
                    send_sem=send_sem.at[len(copies)],
                    recv_sem=recv_sem.at[len(copies)],
                    device_id={axis: lax.rem(lax.axis_index(axis) + k, n)},
                    device_id_type=MESH,
                )
                copy.start()
                copies.append(copy)
        for copy in copies:
            copy.wait()

    got = remote_call(kernel, out_shape, operands, n_sems, collective_id)
    results = []
    for (array, _, spread), n, out in zip(jobs, sizes, got):
        own = array if spread else array[0]
        results.append([own] + [out[k] for k in range(n - 1)])
    return results


def deliver(layers, collective_id):
    width, cores = lax.axis_size("tensor"), lax.axis_size("section")
    block = layers[0].shape[1:]
    out_shape = [jax.ShapeDtypeStruct((cores * width,) + block, layers[0].dtype)]

    def kernel(*refs):
        sources, (target, send_sem, recv_sem, local_sem) = refs[:cores], refs[cores:]
        core, lane = lax.axis_index("section"), lax.axis_index("tensor")

        def device(hop, k):
            return {
                "section": lax.rem(core + hop, cores), "tensor": lax.rem(lane + k, width)
            }

        pairs = [(h, k) for h in range(cores) for k in range(width) if h + k > 0]
        greet([device(h, k) for h, k in pairs])

        def send(layer, hop, k):
            return pltpu.make_async_remote_copy(
                src_ref=sources[layer].at[k],
                dst_ref=target.at[hop * width + k],
                send_sem=send_sem.at[hop * width + k],
                recv_sem=recv_sem.at[hop * width + k],
                device_id=device(hop, k),
                device_id_type=MESH,
            )

        for layer in range(cores):
            for hop in range(cores):
                @pl.when(lax.rem(core + hop, cores) == layer)
                def _():
                    for k in range(width):
                        if hop + k > 0:
                            send(layer, hop, k).start()
                        else:
                            pltpu.make_async_copy(
                                sources[layer].at[0], target.at[0], local_sem
                            ).start()
        for hop, k in pairs:
            send(0, hop, k).wait()
        pltpu.make_async_copy(sources[0].at[0], target.at[0], local_sem).wait()

    anywhere = pl.BlockSpec(memory_space=pl.ANY)
    sems = pltpu.SemaphoreType.DMA((cores * width,))
    out = pl.pallas_call(
        kernel,
        out_shape=out_shape,
        in_specs=[anywhere] * cores,
        out_specs=[anywhere],
        scratch_shapes=[sems, sems, pltpu.SemaphoreType.DMA],
        compiler_params=pltpu.CompilerParams(collective_id=collective_id, has_side_effects=True),
    )(*layers)[0]
    return out.reshape((cores, width) + block)


def turned(stack, start):
    n = stack.shape[0]
    return lax.dynamic_slice_in_dim(jnp.concatenate([stack, stack], axis=0), start, n, axis=0)


def in_order(stack, me):
    n = stack.shape[0]
    return turned(stack[::-1], n - 1 - me)


def per_device(
    tokens, dest_slot, doc_reset, norm_gain, w_in, w_step, step_bias, a_log, d_skip, out_gain, w_out
):
    f32, bf16 = jnp.float32, jnp.bfloat16
    groups = lax.axis_size("dp")
    width = lax.axis_size("tensor")
    cores = lax.axis_size("section")
    group, lane, core = lax.axis_index("dp"), lax.axis_index("tensor"), lax.axis_index("section")
    row_count, feat_local = tokens.shape
    feats = feat_local * width
    depth = w_in.shape[1]
    head_cols = HEADS_DEV * HEAD_DIM
    half = row_count // cores
    src_few = half // width
    few = half // (CHUNKS * width)
    part = few * width

    w_in = lax.all_gather(w_in, "section", axis=0, tiled=True)
    w_out = lax.all_gather(w_out, "section", axis=0, tiled=True)
    step_own = lax.dynamic_slice_in_dim(w_step[0], group * depth, depth, axis=0)
    small = [norm_gain[0], step_bias[0], a_log[0], d_skip[0], out_gain[0]]
    joined = jnp.concatenate(small)[None]

    mine = lax.dynamic_slice_in_dim(tokens, core * half, half, axis=0)
    mine = turned(mine.reshape(width, src_few, feat_local), lane)
    jobs = [
        (mine, "tensor", False), (dest_slot[None], "dp", True),
        (joined, "section", True), (step_own, "section", True),
    ]
    mine, slots, joined, steps = exchange(jobs, 0)

    def by_layer(pair):
        return [jnp.where(core == layer, pair[0], pair[1]) for layer in range(cores)]

    w_step, joined = by_layer(steps), by_layer(joined)
    params, at = [], 0
    for piece in small:
        params.append([j[0, at : at + piece.shape[0]] for j in joined])
        at += piece.shape[0]
    norm_gain, step_bias, a_log, d_skip, out_gain = params

    mine = in_order(jnp.stack(mine), lane)
    mine = mine.transpose(1, 0, 2).reshape(src_few, groups, depth).transpose(1, 0, 2)
    (mine,) = exchange([(turned(mine, group), "dp", False)], 1)
    (parts,) = exchange([(jnp.stack(mine), "tensor", True)], 2)
    (pool,) = exchange([(jnp.stack(parts), "section", True)], 3)
    pool = jnp.stack(pool).reshape(-1, depth)

    slots = in_order(jnp.stack(slots), group).reshape(-1)
    wanted_group = lax.rem(group + jnp.arange(groups), groups)
    wanted = (
        wanted_group[None, :, None] * row_count
        + jnp.arange(CHUNKS)[:, None, None] * (cores * part)
        + core * part
        + jnp.arange(part)[None, None, :]
    ).reshape(-1)
    everyrow = jnp.arange(slots.shape[0], dtype=jnp.int32)
    source_of = jnp.sum(
        jnp.where(slots[None, :] == wanted[:, None], everyrow[None, :], 0), axis=1
    )
    src_group, inner = source_of // row_count, source_of % row_count
    src_core, inner = inner // half, inner % half
    src_lane, inner = inner // src_few, inner % src_few
    place = (core - src_core) % cores * width + (lane - src_lane) % width
    place = (place * groups + (group - src_group) % groups) * src_few + inner
    first = pool[place].reshape(CHUNKS, groups, part, depth)
    gain_own = lax.dynamic_slice_in_dim(norm_gain[0], group * depth, depth)

    def project(rows, layer):
        flat = rows.reshape(groups * part, depth)
        proj = jnp.dot(flat, w_in[layer], preferred_element_type=f32).astype(bf16)
        pre = jnp.dot(flat, w_step[layer], preferred_element_type=f32)
        return proj.reshape(groups, part, -1), pre.reshape(groups, part, -1)

    def added(blocks):
        return sum(b.astype(f32) for b in blocks)

    def mix(proj, pre, resets, state, layer):
        proj = lax.all_gather(proj, "section", axis=0, tiled=True)
        pre = lax.all_gather(pre, "section", axis=0, tiled=True)
        count = proj.shape[0]
        step_size = jax.nn.softplus(pre + step_bias[layer])
        log_decay = -jnp.exp(a_log[layer]) * step_size
        mixed, state = scan_block(
            proj[:, head_cols : 2 * head_cols].reshape(count, HEADS_DEV, HEAD_DIM),
            proj[:, 2 * head_cols : 2 * head_cols + STATE],
            proj[:, 2 * head_cols + STATE :],
            step_size,
            log_decay,
            resets,
            state,
            d_skip[layer],
        )
        mixed = mixed.reshape(count, head_cols)
        mixed = lax.dynamic_slice_in_dim(mixed, core * part, part, axis=0)
        gate = lax.dynamic_slice_in_dim(proj[:, :head_cols], core * part, part, axis=0).astype(f32)
        gated = mixed * jax.nn.silu(gate)
        meansq_out = jnp.mean(gated * gated, axis=-1, keepdims=True)
        normed = (gated * lax.rsqrt(meansq_out + epsilon) * out_gain[layer]).astype(bf16)
        normed = turned(normed.reshape(width, few, head_cols), lane).reshape(part, head_cols)
        partial_value = jnp.dot(normed, w_out[layer], preferred_element_type=f32).astype(bf16)
        return (partial_value.reshape(width, few, feats), "tensor", False), state

    resets = doc_reset.reshape(CHUNKS, -1)

    def project_first(c):
        wide = first[c].astype(f32)
        squares = jnp.sum(wide * wide, axis=-1)
        proj, pre = project((wide * gain_own).astype(bf16), 0)
        side = jnp.concatenate([pre, squares[:, :, None]], axis=-1)
        kept = lax.dynamic_slice_in_dim(first[c], lane * few, few, axis=1)
        return [(proj, "dp", False), (side, "dp", False), (kept, "dp", False)]

    def mix_first(got, c, state):
        proj, side, kept = got
        side = added(side)
        scale = lax.rsqrt(side[:, HEADS_DEV:] / feats + epsilon)
        job, state = mix(
            (added(proj) * scale).astype(bf16), side[:, :HEADS_DEV] * scale, resets[c], state, 0
        )
        kept = in_order(jnp.stack(kept), group).transpose(1, 0, 2).reshape(few, feats)
        return job, state, kept

    def next_input(kept, got):
        rows = (kept.astype(f32) + added(got)).astype(bf16)
        widened = rows.astype(f32)
        meansq = jnp.mean(widened * widened, axis=-1, keepdims=True)
        u = (widened * lax.rsqrt(meansq + epsilon) * norm_gain[1]).astype(bf16)
        u = turned(u.reshape(few, groups, depth).transpose(1, 0, 2), group)
        return rows, (u, "dp", False)

    def project_next(got):
        proj, pre = project(jnp.stack(got, axis=1), 1)
        back = [(groups - k) % groups for k in range(groups)]
        return [
            (jnp.stack([proj[k] for k in back]), "dp", False),
            (jnp.stack([pre[k] for k in back]), "dp", False),
        ]

    def mix_next(got, c, state):
        proj, pre = got
        proj = in_order(added(proj).astype(bf16).reshape(width, few, -1), lane).reshape(part, -1)
        pre = in_order(added(pre).reshape(width, few, -1), lane).reshape(part, -1)
        return mix(proj, pre, resets[c], state, 1)

    start = jnp.zeros((HEADS_DEV, HEAD_DIM, STATE), f32)
    got = exchange(project_first(0), 4)
    out_a, state, kept_a = mix_first(got, 0, start)
    *got, sum_a = exchange(project_first(1) + [out_a], 5)
    rows_a, u_a = next_input(kept_a, sum_a)
    out_b, state, kept_b = mix_first(got, 1, state)
    u_a, sum_b = exchange([u_a, out_b], 6)
    rows_b, u_b = next_input(kept_b, sum_b)
    full_a, u_b = exchange([(jnp.stack(u_a), "tensor", True), u_b], 7)
    *got, full_b = exchange(project_next(full_a) + [(jnp.stack(u_b), "tensor", True)], 8)
    out_a, state = mix_next(got, 0, start)
    *got, sum_a = exchange(project_next(full_b) + [out_a], 9)
    last_a = (rows_a.astype(f32) + added(sum_a)).astype(bf16)
    out_b, state = mix_next(got, 1, state)
    (sum_b,) = exchange([out_b], 10)
    last_b = (rows_b.astype(f32) + added(sum_b)).astype(bf16)

    def for_lanes(a, b):
        both = jnp.stack([a, b]).reshape(CHUNKS, few, width, feat_local).transpose(2, 0, 1, 3)
        return turned(both, lane)

    out = deliver([for_lanes(rows_a, rows_b), for_lanes(last_a, last_b)], 11)
    out = jnp.stack([in_order(out[hop], lane) for hop in range(cores)])
    out = in_order(out, core).transpose(2, 0, 1, 3, 4)
    return out.reshape(1, row_count, feat_local)


def solution(mesh):
    placed = (
        P("dp", "tensor"),
        P("dp"),
        P("dp"),
        P("section", None),
        P("section", "dp", "tensor"),
        P("section", None, "tensor"),
        P("section", "tensor"),
        P("section", "tensor"),
        P("section", "tensor"),
        P("section", "tensor"),
        P("section", "tensor", None),
    )
    return jax.shard_map(
        per_device,
        mesh=mesh,
        in_specs=placed,
        out_specs=P("section", "dp", "tensor"),
        check_vma=False,
    )
```

```python
import jax
import jax.numpy as jnp
from jax import lax
from jax.experimental import pallas as pl
from jax.experimental.pallas import tpu as pltpu
from jax.sharding import PartitionSpec as P

HEAD_DIM = 64
STATE = 128
HEADS_DEV = 8


epsilon = 1e-05


def scan_block(inputs, writes, readout, step_size, log_decay, resets, state, skips):
    segment = jnp.cumsum(resets)
    cumulative = jnp.cumsum(log_decay, axis=0)
    positions = jnp.arange(resets.shape[0])
    in_segment = (segment[:, None] == segment[None, :]) & (positions[:, None] >= positions[None, :])
    by_head = cumulative.T
    gap = by_head[:, :, None] - by_head[:, None, :]
    decayed = jnp.where(in_segment[None], jnp.exp(jnp.where(in_segment[None], gap, 0.0)), 0.0)
    f32 = jnp.float32
    scores = jnp.einsum("tn,sn->ts", readout, writes, preferred_element_type=f32)
    weights = scores[None] * decayed * step_size.T[:, None, :]
    output = jnp.einsum("hts,shp->thp", weights, inputs.astype(f32))
    carry_ok = (segment == 0).astype(f32)
    carried = jnp.einsum("tn,hpn->thp", readout.astype(f32), state)
    output = output + carry_ok[:, None, None] * jnp.exp(cumulative)[:, :, None] * carried
    last_seg = segment[-1]
    tail = (
        (segment == last_seg).astype(f32)[:, None]
        * jnp.exp(cumulative[-1][None, :] - cumulative)
        * step_size
    )
    fresh = jnp.einsum("shp,sn->hpn", tail[:, :, None] * inputs.astype(f32), writes.astype(f32))
    kept = (last_seg == 0).astype(f32) * jnp.exp(cumulative[-1])[:, None, None] * state
    output = output + skips[None, :, None] * inputs.astype(f32)
    return (output, fresh + kept)


CHUNKS = 2


MESH = pl.DeviceIdType.MESH


def greet(peers):
    barrier = pltpu.get_barrier_semaphore()
    for peer in peers:
        pl.semaphore_signal(barrier, inc=1, device_id=peer, device_id_type=MESH)
    pl.semaphore_wait(barrier, len(peers))


def remote_call(kernel, out_shape, operands, n_sems, collective_id):
    anywhere = pl.BlockSpec(memory_space=pl.ANY)
    sems = [pltpu.SemaphoreType.DMA((n_sems,)), pltpu.SemaphoreType.DMA((n_sems,))]
    return pl.pallas_call(
        kernel,
        out_shape=out_shape,
        in_specs=[anywhere] * len(operands),
        out_specs=[anywhere] * len(out_shape),
        scratch_shapes=sems,
        compiler_params=pltpu.CompilerParams(collective_id=collective_id, has_side_effects=True),
    )(*operands)


def send_all(jobs, collective_id):
    sizes = [lax.axis_size(axis) for _, axis, _ in jobs]
    operands = [array for array, _, _ in jobs]
    out_shape = []
    for (array, _, spread), n in zip(jobs, sizes):
        block = array.shape if spread else array.shape[1:]
        out_shape.append(jax.ShapeDtypeStruct((n - 1,) + block, array.dtype))
    axes = sorted({axis for _, axis, _ in jobs})
    n_sems = sum(n - 1 for n in sizes)

    def kernel(*refs):
        sources, targets = refs[: len(jobs)], refs[len(jobs) : 2 * len(jobs)]
        send_sem, recv_sem = refs[2 * len(jobs) :]
        peers = []
        for axis in axes:
            n = lax.axis_size(axis)
            peers += [{axis: lax.rem(lax.axis_index(axis) + k, n)} for k in range(1, n)]
        greet(peers)
        copies = []
        for (_, axis, spread), n, source, target in zip(jobs, sizes, sources, targets):
            for k in range(1, n):
                copy = pltpu.make_async_remote_copy(
                    src_ref=source if spread else source.at[k],
                    dst_ref=target.at[k - 1],
                    send_sem=send_sem.at[len(copies)],
                    recv_sem=recv_sem.at[len(copies)],
                    device_id={axis: lax.rem(lax.axis_index(axis) + k, n)},
                    device_id_type=MESH,
                )
                copy.start()
                copies.append(copy)
        for copy in copies:
            copy.wait()

    got = remote_call(kernel, out_shape, operands, n_sems, collective_id)
    results = []
    for (array, _, spread), n, out in zip(jobs, sizes, got):
        own = array if spread else array[0]
        results.append([own] + [out[k] for k in range(n - 1)])
    return results


def deliver(layers, collective_id):
    width, cores = lax.axis_size("tensor"), lax.axis_size("section")
    block = layers[0].shape[1:]
    out_shape = [jax.ShapeDtypeStruct((cores * width,) + block, layers[0].dtype)]

    def kernel(*refs):
        sources, (target, send_sem, recv_sem, local_sem) = refs[:cores], refs[cores:]
        core, lane = lax.axis_index("section"), lax.axis_index("tensor")

        def device(hop, k):
            return {
                "section": lax.rem(core + hop, cores), "tensor": lax.rem(lane + k, width)
            }

        pairs = [(h, k) for h in range(cores) for k in range(width) if h + k > 0]
        greet([device(h, k) for h, k in pairs])

        def send(layer, hop, k):
            return pltpu.make_async_remote_copy(
                src_ref=sources[layer].at[k],
                dst_ref=target.at[hop * width + k],
                send_sem=send_sem.at[hop * width + k],
                recv_sem=recv_sem.at[hop * width + k],
                device_id=device(hop, k),
                device_id_type=MESH,
            )

        for layer in range(cores):
            for hop in range(cores):
                @pl.when(lax.rem(core + hop, cores) == layer)
                def _():
                    for k in range(width):
                        if hop + k > 0:
                            send(layer, hop, k).start()
                        else:
                            pltpu.make_async_copy(
                                sources[layer].at[0], target.at[0], local_sem
                            ).start()
        for hop, k in pairs:
            send(0, hop, k).wait()
        pltpu.make_async_copy(sources[0].at[0], target.at[0], local_sem).wait()

    anywhere = pl.BlockSpec(memory_space=pl.ANY)
    sems = pltpu.SemaphoreType.DMA((cores * width,))
    out = pl.pallas_call(
        kernel,
        out_shape=out_shape,
        in_specs=[anywhere] * cores,
        out_specs=[anywhere],
        scratch_shapes=[sems, sems, pltpu.SemaphoreType.DMA],
        compiler_params=pltpu.CompilerParams(collective_id=collective_id, has_side_effects=True),
    )(*layers)[0]
    return out.reshape((cores, width) + block)


def shift(block, axis, distance):
    n = lax.axis_size(axis)
    return lax.ppermute(block, axis, [(i, (i + distance) % n) for i in range(n)])


def exchange(blocks, axis):
    return [b if k == 0 else shift(b, axis, k) for k, b in enumerate(blocks)]


def turned(stack, start):
    n = stack.shape[0]
    return lax.dynamic_slice_in_dim(jnp.concatenate([stack, stack], axis=0), start, n, axis=0)


def in_order(stack, me):
    n = stack.shape[0]
    return turned(stack[::-1], n - 1 - me)


def per_device(
    tokens, dest_slot, doc_reset, norm_gain, w_in, w_step, step_bias, a_log, d_skip, out_gain, w_out
):
    f32, bf16 = jnp.float32, jnp.bfloat16
    groups = lax.axis_size("dp")
    width = lax.axis_size("tensor")
    cores = lax.axis_size("section")
    group, lane, core = lax.axis_index("dp"), lax.axis_index("tensor"), lax.axis_index("section")
    row_count, feat_local = tokens.shape
    feats = feat_local * width
    depth = w_in.shape[1]
    head_cols = HEADS_DEV * HEAD_DIM
    half = row_count // cores
    src_few = half // width
    few = half // (CHUNKS * width)
    part = few * width

    w_in = lax.all_gather(w_in, "section", axis=0, tiled=True)
    w_out = lax.all_gather(w_out, "section", axis=0, tiled=True)
    step_own = lax.dynamic_slice_in_dim(w_step[0], group * depth, depth, axis=0)
    small = [norm_gain[0], step_bias[0], a_log[0], d_skip[0], out_gain[0]]
    joined = jnp.concatenate(small)[None]

    mine = lax.dynamic_slice_in_dim(tokens, core * half, half, axis=0)
    mine = turned(mine.reshape(width, src_few, feat_local), lane)
    jobs = [
        (mine, "tensor", False), (dest_slot[None], "dp", True),
        (joined, "section", True), (step_own, "section", True),
    ]
    mine, slots, joined, steps = send_all(jobs, 0)

    def by_layer(pair):
        return [jnp.where(core == layer, pair[0], pair[1]) for layer in range(cores)]

    w_step, joined = by_layer(steps), by_layer(joined)
    params, at = [], 0
    for piece in small:
        params.append([j[0, at : at + piece.shape[0]] for j in joined])
        at += piece.shape[0]
    norm_gain, step_bias, a_log, d_skip, out_gain = params

    mine = in_order(jnp.stack(mine), lane)
    mine = mine.transpose(1, 0, 2).reshape(src_few, groups, depth).transpose(1, 0, 2)
    (mine,) = send_all([(turned(mine, group), "dp", False)], 1)
    (parts,) = send_all([(jnp.stack(mine), "tensor", True)], 2)
    (pool,) = send_all([(jnp.stack(parts), "section", True)], 3)
    pool = jnp.stack(pool).reshape(-1, depth)

    slots = in_order(jnp.stack(slots), group).reshape(-1)
    wanted_group = lax.rem(group + jnp.arange(groups), groups)
    wanted = (
        wanted_group[None, :, None] * row_count
        + jnp.arange(CHUNKS)[:, None, None] * (cores * part)
        + core * part
        + jnp.arange(part)[None, None, :]
    ).reshape(-1)
    everyrow = jnp.arange(slots.shape[0], dtype=jnp.int32)
    source_of = jnp.sum(
        jnp.where(slots[None, :] == wanted[:, None], everyrow[None, :], 0), axis=1
    )
    src_group, inner = source_of // row_count, source_of % row_count
    src_core, inner = inner // half, inner % half
    src_lane, inner = inner // src_few, inner % src_few
    place = (core - src_core) % cores * width + (lane - src_lane) % width
    place = (place * groups + (group - src_group) % groups) * src_few + inner
    first = pool[place].reshape(CHUNKS, groups, part, depth)
    gain_own = lax.dynamic_slice_in_dim(norm_gain[0], group * depth, depth)

    def project(rows, layer):
        flat = rows.reshape(groups * part, depth)
        proj = jnp.dot(flat, w_in[layer], preferred_element_type=f32).astype(bf16)
        pre = jnp.dot(flat, w_step[layer], preferred_element_type=f32)
        return proj.reshape(groups, part, -1), pre.reshape(groups, part, -1)

    def packed(proj, side):
        high = lax.reduce_precision(side, 8, 7)
        low = lax.reduce_precision(side - high, 8, 7)
        return jnp.concatenate([proj, high.astype(bf16), low.astype(bf16)], axis=-1)

    def unpacked(total):
        cols = w_in.shape[-1]
        extra = (total.shape[-1] - cols) // 2
        return total[:, :cols], total[:, cols : cols + extra] + total[:, cols + extra :]

    def added(blocks):
        return sum(b.astype(f32) for b in blocks)

    def mix(proj, pre, resets, state, layer):
        proj = lax.all_gather(proj, "section", axis=0, tiled=True)
        pre = lax.all_gather(pre, "section", axis=0, tiled=True)
        count = proj.shape[0]
        step_size = jax.nn.softplus(pre + step_bias[layer])
        log_decay = -jnp.exp(a_log[layer]) * step_size
        mixed, state = scan_block(
            proj[:, head_cols : 2 * head_cols].reshape(count, HEADS_DEV, HEAD_DIM),
            proj[:, 2 * head_cols : 2 * head_cols + STATE],
            proj[:, 2 * head_cols + STATE :],
            step_size,
            log_decay,
            resets,
            state,
            d_skip[layer],
        )
        mixed = mixed.reshape(count, head_cols)
        mixed = lax.dynamic_slice_in_dim(mixed, core * part, part, axis=0)
        gate = lax.dynamic_slice_in_dim(proj[:, :head_cols], core * part, part, axis=0).astype(f32)
        gated = mixed * jax.nn.silu(gate)
        meansq_out = jnp.mean(gated * gated, axis=-1, keepdims=True)
        normed = (gated * lax.rsqrt(meansq_out + epsilon) * out_gain[layer]).astype(bf16)
        normed = turned(normed.reshape(width, few, head_cols), lane).reshape(part, head_cols)
        partial_value = jnp.dot(normed, w_out[layer], preferred_element_type=f32).astype(bf16)
        blocks = partial_value.reshape(width, few, feats)
        return added(exchange([blocks[k] for k in range(width)], "tensor")), state

    resets = doc_reset.reshape(CHUNKS, -1)
    zero_state = jnp.zeros((HEADS_DEV, HEAD_DIM, STATE), f32)
    sent = []
    for c in range(CHUNKS):
        wide = first[c].astype(f32)
        squares = jnp.sum(wide * wide, axis=-1)
        proj, pre = project((wide * gain_own).astype(bf16), 0)
        side = jnp.concatenate([pre, squares[:, :, None]], axis=-1)
        kept = lax.dynamic_slice_in_dim(first[c], lane * few, few, axis=1)
        proj = packed(proj, side)
        proj = exchange([proj[k] for k in range(groups)], "dp")
        kept = exchange([kept[k] for k in range(groups)], "dp")
        sent.append((proj, kept))
    state = zero_state
    middle, outs = [], []
    for c in range(CHUNKS):
        proj, kept = sent[c]
        proj, side = unpacked(added(proj))
        scale = lax.rsqrt(side[:, HEADS_DEV:] / feats + epsilon)
        summed, state = mix(
            (proj * scale).astype(bf16), side[:, :HEADS_DEV] * scale, resets[c], state, 0
        )
        kept = in_order(jnp.stack(kept), group).transpose(1, 0, 2).reshape(few, feats)
        rows = (kept.astype(f32) + summed).astype(bf16)
        middle.append(rows)
        widened = rows.astype(f32)
        meansq = jnp.mean(widened * widened, axis=-1, keepdims=True)
        u = (widened * lax.rsqrt(meansq + epsilon) * norm_gain[1]).astype(bf16)
        u = turned(u.reshape(few, groups, depth).transpose(1, 0, 2), group)
        u = jnp.stack(exchange([u[k] for k in range(groups)], "dp"))
        u = jnp.stack(exchange([u] * width, "tensor"), axis=1)
        proj, pre = project(u, 1)
        back = [(groups - k) % groups for k in range(groups)]
        both = packed(proj, pre)
        sent[c] = exchange([both[k] for k in back], "dp")
    state = zero_state
    for c in range(CHUNKS):
        proj, pre = unpacked(added(sent[c]))
        proj = in_order(proj.astype(bf16).reshape(width, few, -1), lane).reshape(part, -1)
        pre = in_order(pre.reshape(width, few, -1), lane).reshape(part, -1)
        summed, state = mix(proj, pre, resets[c], state, 1)
        rows = (middle[c].astype(f32) + summed).astype(bf16)
        outs.append(rows)

    def for_lanes(rows):
        both = jnp.stack(rows).reshape(CHUNKS, few, width, feat_local).transpose(2, 0, 1, 3)
        return turned(both, lane)

    out = deliver([for_lanes(middle), for_lanes(outs)], 4)
    out = jnp.stack([in_order(out[hop], lane) for hop in range(cores)])
    out = in_order(out, core).transpose(2, 0, 1, 3, 4)
    return out.reshape(1, row_count, feat_local)


def solution(mesh):
    placed = (
        P("dp", "tensor"),
        P("dp"),
        P("dp"),
        P("section", None),
        P("section", "dp", "tensor"),
        P("section", None, "tensor"),
        P("section", "tensor"),
        P("section", "tensor"),
        P("section", "tensor"),
        P("section", "tensor"),
        P("section", "tensor", None),
    )
    return jax.shard_map(
        per_device,
        mesh=mesh,
        in_specs=placed,
        out_specs=P("section", "dp", "tensor"),
        check_vma=False,
    )
```
